32 devices in a mesh: groups: 2 (over y), clip: 4 (over z), strip: 4 (over x, core).
Axes of the slice: x: 2, y: 2, z: 4, core: 2. Of those that a mesh axis runs over, the one named last changes fastest.
Arguments:
- latents: bfloat16 [32, 20, 64, 320], P(('groups', 'clip'), 'strip'), parts along dimension 0, may hold values from -6 to 6
- anchor_index: int32 [8, 1], P(('groups', 'clip')), parts along dimension 0, may hold values from 0 to 3
- window: int32 [1], replicated, may hold values from 2 to 4
- gain_one: float32 [320], replicated, may hold values from 0.5 to 1.5
- spatial_w: bfloat16 [3, 3, 320, 320], replicated, may hold values from -0.109375 to 0.109375
- gain_two: float32 [320], replicated, may hold values from 0.5 to 1.5
- temporal_w: bfloat16 [3, 320, 320], replicated, may hold values from -0.1875 to 0.1875
- gain_three: float32 [320], replicated, may hold values from 0.5 to 1.5
- w_query: bfloat16 [320, 320], replicated
- w_keyval: bfloat16 [320, 640], replicated
- w_out: bfloat16 [320, 320], replicated, may hold values from -0.3125 to 0.3125
Outputs:
- block_out: bfloat16 [32, 20, 64, 320], P(('groups', 'clip'), 'strip'), parts along dimension 0
The draws below stay inside these ranges and needn't reach their ends.
There are 2 independent parts, one for each index of `groups`. The reference program is written for one: setup_inputs(seed, part) draws one part's arguments, and reference() takes and returns one part's arrays. A program takes and returns all parts, laid end to end along the dimension named above; an argument that names none is the same for every part. Nothing has to cross between parts.
Inputs may be any that keep to these rules, and one draw needn't show every extreme that they name: `anchor_index`: indices of anchor frames within their clip of 4 frames. Frames closer than window[0] within one clip attend to each other.
All inputs are finite; a program needn't handle non-finite values.
Results may differ from the reference program's by a relative error of at most 0.0085.
Values may be sent and summed in bfloat16 or wider, within the bound.
A program may use at most 128 MiB of HBM per device.

```python
import math
import jax
import jax.numpy as jnp
from jax import lax

C = 320
HEADS = 5
HEAD_DIM = 64
FR_DEV = 4
WIDTH = 64
NANC = 1
CLIPS = 4
FRAMES = 16
HEIGHT = 20


def query_key_parts(key):
    own_query = jax.random.normal(jax.random.fold_in(key, 12), (C, C), jnp.float32)
    own_key = jax.random.normal(jax.random.fold_in(key, 13), (C, C), jnp.float32)
    query_part = own_query
    key_part = own_key
    return (query_part / math.sqrt(C), key_part / math.sqrt(C))


def draw_w_query(key, part):
    return query_key_parts(key)[0].astype(jnp.bfloat16)


def draw_w_keyval(key, part):
    key_part = query_key_parts(key)[1]
    value_part = jax.random.normal(jax.random.fold_in(key, 14), (C, C), jnp.float32) / math.sqrt(C)
    return jnp.concatenate([key_part, value_part], axis=1).astype(jnp.bfloat16)


def with_ends(result, key, least, largest):
    extent = result.shape
    spot = [jax.random.randint(jax.random.fold_in(key, axis), (), 0, extent[axis]) for axis in range(len(extent))]
    result = result.at[tuple(spot)].set(least)
    longest = extent.index(max(extent))
    spot[longest] = (spot[longest] + 1) % extent[longest]
    return result.at[tuple(spot)].set(largest)


def shard_levels(key, dims, cuts, least, high):
    def one(dim, shards_of):
        steps = jax.random.uniform(jax.random.fold_in(jax.random.fold_in(key, 6), dim), (shards_of,), jnp.float32, least / len(cuts), high / len(cuts))
        return jnp.repeat(jnp.exp(steps), dims[dim] // shards_of).reshape((-1,) + (1,) * (len(dims) - dim - 1))

    loudness = one(*cuts[0])
    for cut in cuts[1:]:
        loudness = loudness * one(*cut)
    return loudness


def noise(rng, extent, spread, bound, pieces=(), kind=jnp.bfloat16):
    level = shard_levels(rng, extent, pieces, -0.22, 0.18) if pieces else 1.0
    entries = jax.random.normal(rng, extent, jnp.float32) * spread * level
    return jnp.minimum(jnp.maximum(entries, -bound), bound).astype(kind)


def setup_inputs(seed: int = 0, part: int = 0) -> dict:
    keys = jax.random.split(jax.random.key(seed), 12)
    part_splits = jax.random.split(jax.random.fold_in(keys[11], part), 12)
    latents = noise(part_splits[0], (FRAMES, HEIGHT, WIDTH, C), 1.0, 6.0, ((0, 4), (1, 4)))
    anchor_index = with_ends(jax.random.randint(part_splits[1], (CLIPS, NANC), 0, FR_DEV), jax.random.fold_in(part_splits[1], 1), 0, FR_DEV - 1).astype(jnp.int32)
    window = jax.random.randint(keys[2], (1,), 2, FR_DEV + 1).astype(jnp.int32)
    gain_one = jnp.clip(jax.random.uniform(keys[3], (C,), jnp.float32, 0.5, 1.5), 0.5, 1.5)
    spatial_w = noise(keys[4], (3, 3, C, C), (9 * C) ** -0.5, 0.109375)
    gain_two = jnp.clip(jax.random.uniform(keys[5], (C,), jnp.float32, 0.5, 1.5), 0.5, 1.5)
    temporal_w = noise(keys[6], (3, C, C), (3 * C) ** -0.5, 0.1875)
    gain_three = jnp.clip(jax.random.uniform(keys[7], (C,), jnp.float32, 0.5, 1.5), 0.5, 1.5)
    w_query = draw_w_query(jax.random.fold_in(keys[11], 71), part)
    w_keyval = draw_w_keyval(jax.random.fold_in(keys[11], 71), part)
    w_out = noise(keys[10], (C, C), C ** -0.5, 0.3125)
    return dict(latents=latents, anchor_index=anchor_index, window=window, gain_one=gain_one, spatial_w=spatial_w, gain_two=gain_two, temporal_w=temporal_w, gain_three=gain_three, w_query=w_query, w_keyval=w_keyval, w_out=w_out)


def layer_norm(values, gain):
    widened = values.astype(jnp.float32)
    centred = widened - lax.optimization_barrier(jnp.mean(widened, axis=-1, keepdims=True))
    variance = lax.optimization_barrier(jnp.mean(centred * centred, axis=-1, keepdims=True))
    return centred * lax.rsqrt(variance + 1e-05) * gain

def reference(latents, anchor_index, window, gain_one, spatial_w, gain_two, temporal_w, gain_three, w_query, w_keyval, w_out):
    frames, height, columns, channels = latents.shape
    hidden_one = jax.nn.silu(layer_norm(latents, gain_one)).astype(jnp.bfloat16)
    padded = jnp.pad(hidden_one, ((0, 0), (1, 1), (1, 1), (0, 0)))
    summed = jnp.zeros(latents.shape, jnp.float32)
    for row_tap in range(3):
        for col_tap in range(3):
            summed = summed + jnp.dot(padded[:, row_tap:row_tap + height, col_tap:col_tap + columns, :], spatial_w[row_tap, col_tap], preferred_element_type=jnp.float32)
    spatial = (latents.astype(jnp.float32) + summed).astype(jnp.bfloat16)
    hidden_two = jax.nn.silu(layer_norm(spatial, gain_two)).astype(jnp.bfloat16)
    padded_two = jnp.pad(hidden_two, ((1, 1), (0, 0), (0, 0), (0, 0)))
    summed = jnp.zeros(latents.shape, jnp.float32)
    for frame_tap in range(3):
        summed = summed + jnp.dot(padded_two[frame_tap:frame_tap + frames], temporal_w[frame_tap], preferred_element_type=jnp.float32)
    temporal = (spatial.astype(jnp.float32) + summed).astype(jnp.bfloat16)
    normed = layer_norm(temporal, gain_three).astype(jnp.bfloat16)
    query = lax.optimization_barrier(jnp.dot(normed, w_query, preferred_element_type=jnp.float32).astype(jnp.bfloat16))
    keyval = lax.optimization_barrier(jnp.dot(normed, w_keyval, preferred_element_type=jnp.float32).astype(jnp.bfloat16))
    clips = anchor_index.shape[0]
    per_clip = frames // clips
    pixels = height * columns
    global_frames = (anchor_index + per_clip * jnp.arange(clips, dtype=jnp.int32)[:, None]).reshape(-1).astype(jnp.int32)
    anchors = jnp.take(keyval, global_frames, axis=0).reshape(-1, pixels, 2, HEADS, HEAD_DIM).astype(jnp.float32)
    anchor_keys = anchors[:, :, 0]
    anchor_values = anchors[:, :, 1]
    query_clips = query.reshape(clips, per_clip, pixels, HEADS, HEAD_DIM)
    keyval_clips = keyval.reshape(clips, per_clip, pixels, 2, HEADS, HEAD_DIM)
    score_scale = 1.0 / math.sqrt(HEAD_DIM)
    places = jnp.arange(per_clip, dtype=jnp.int32)
    inside = jnp.abs(places[:, None] - places[None, :]) < window[0]

    def one_clip(inputs):
        query_part, keyval_part = inputs
        query_wide = query_part.astype(jnp.float32)
        key_wide = keyval_part[:, :, 0].astype(jnp.float32)
        value_wide = keyval_part[:, :, 1].astype(jnp.float32)
        nearby = jnp.einsum('iphd,jphd->phij', query_wide, key_wide) * score_scale
        nearby = jnp.where(inside, nearby, -jnp.inf)
        remote = jnp.einsum('iphd,aphd->phia', query_wide, anchor_keys) * score_scale
        scores = jnp.concatenate([nearby, remote], axis=-1)
        maxima = lax.optimization_barrier(jnp.max(scores, axis=-1, keepdims=True))
        weights = jnp.exp(scores - maxima)
        probs = lax.optimization_barrier((weights / lax.optimization_barrier(jnp.sum(weights, axis=-1, keepdims=True))).astype(jnp.bfloat16)).astype(jnp.float32)
        mixed = jnp.einsum('phij,jphd->iphd', probs[..., :per_clip], value_wide) + jnp.einsum('phia,aphd->iphd', probs[..., per_clip:], anchor_values)
        return mixed.astype(jnp.bfloat16)
    attended = lax.map(one_clip, (query_clips, keyval_clips))
    attended = attended.reshape(frames, height, columns, channels)
    block_out = temporal.astype(jnp.float32) + jnp.dot(attended, w_out, preferred_element_type=jnp.float32)
    return block_out.astype(jnp.bfloat16)
```

```python
import functools
import math

import jax
import jax.numpy as jnp
from jax import lax
from jax.experimental import pallas as pl
from jax.experimental.pallas import tpu as pltpu
from jax.sharding import PartitionSpec as P

HEAD_DIM = 64
MESH = pl.DeviceIdType.MESH
F32 = jnp.float32
BF16 = jnp.bfloat16


def norm_rows(values, gain):
    inv = 1.0 / values.shape[0]
    centred = values - jnp.sum(values, axis=0, keepdims=True) * inv
    variance = jnp.sum(centred * centred, axis=0, keepdims=True) * inv
    return centred * lax.rsqrt(variance + 1e-05) * gain


def silu(u):
    return u / (1.0 + jnp.exp(-u))


def kernel(
    dims,
    latents, anchor_index, window, gain_one, spatial_w, gain_two, temporal_w, gain_three,
    w_query, w_keyval, w_out,
    out,
    lat, sw, tw, wq, wkv, wo, swt, twt, wqkvt, wot, gains,
    rim, taps, base, spatial, hidden, temporal, qkv, sent, clip_rim, anchors,
    local_sem, rim_send, rim_recv, clip_send, clip_recv, anchor_send, anchor_recv,
):
    frames, rows, columns, channels, strips, clips, picks = dims
    lanes = frames * columns
    half = channels // 2
    heads = channels // HEAD_DIM
    strip = lax.axis_index("strip")
    clip = lax.axis_index("clip")
    has_up, has_down = strip > 0, strip < strips - 1
    has_before, has_after = clip > 0, clip < clips - 1

    loads = [
        pltpu.make_async_copy(src, dst, local_sem.at[i])
        for i, (src, dst) in enumerate(
            ((latents, lat), (spatial_w, sw), (temporal_w, tw), (w_query, wq), (w_keyval, wkv), (w_out, wo))
        )
    ]
    for load in loads:
        load.start()

    barrier = pltpu.get_barrier_semaphore()

    @pl.when(has_up)
    def _():
        pl.semaphore_signal(barrier, inc=1, device_id={"strip": strip - 1}, device_id_type=MESH)

    @pl.when(has_down)
    def _():
        pl.semaphore_signal(barrier, inc=1, device_id={"strip": strip + 1}, device_id_type=MESH)

    others = [lax.rem(clip + d, clips) for d in range(1, clips)]
    for other in others:
        pl.semaphore_signal(barrier, inc=1, device_id={"clip": other}, device_id_type=MESH)
    pl.semaphore_wait(barrier, clips - 1 + has_up.astype(jnp.int32) + has_down.astype(jnp.int32))

    def rim_copy(side):
        source = latents.at[:, 0] if side == 1 else latents.at[:, rows - 1]
        return pltpu.make_async_remote_copy(
            src_ref=source, dst_ref=rim.at[side], send_sem=rim_send.at[side], recv_sem=rim_recv.at[side],
            device_id={"strip": strip - 1 if side == 1 else strip + 1}, device_id_type=MESH,
        )

    pl.when(has_up)(lambda: rim_copy(1).start())
    pl.when(has_down)(lambda: rim_copy(0).start())

    lane = lax.broadcasted_iota(jnp.int32, (1, lanes), 1)
    column = lax.rem(lane, columns)
    frame = lane // columns
    lane_half = lax.broadcasted_iota(jnp.int32, (1, 2 * columns), 1)
    low = lane_half < columns

    for i, ref in enumerate((gain_one, gain_two, gain_three)):
        gains[i] = jnp.broadcast_to(ref[...], (lanes, channels)).T

    def put_taps(slot, turned):
        wide = silu(norm_rows(turned, gains[0]))
        left = jnp.where(column == 0, 0.0, pltpu.roll(wide, 1, 1))
        right = jnp.where(column == columns - 1, 0.0, pltpu.roll(wide, lanes - 1, 1))
        taps[slot, 0:channels] = left.astype(BF16)
        taps[slot, channels : 2 * channels] = wide.astype(BF16)
        taps[slot, 2 * channels :] = right.astype(BF16)

    loads[0].wait()

    @pl.loop(0, rows)
    def _(r):
        turned = lat[:, r].reshape(lanes, channels).astype(F32).T
        base[r] = turned.astype(BF16)
        put_taps(r + 1, turned)

    loads[1].wait()
    for a in range(3):
        swt[a] = sw[a].reshape(3 * channels, channels).astype(F32).T.astype(BF16)
    for load in loads[2:]:
        load.wait()
    twt[...] = tw[...].reshape(3 * channels, channels).astype(F32).T.astype(BF16)
    wqkvt[0:channels] = wq[...].astype(F32).T.astype(BF16)
    wqkvt[channels:] = wkv[...].astype(F32).T.astype(BF16)
    wot[...] = wo[...].astype(F32).T.astype(BF16)

    def put_rim(side, slot, present):
        @pl.when(present)
        def _():
            rim_copy(side).wait_recv()
            put_taps(slot, rim[side].reshape(lanes, channels).astype(F32).T)

        @pl.when(jnp.logical_not(present))
        def _():
            taps[slot] = jnp.zeros(taps.shape[1:], BF16)

    def swap(values):
        return pltpu.roll(values, columns, 1)

    def clip_copy(side, r):
        return pltpu.make_async_remote_copy(
            src_ref=sent.at[side, r], dst_ref=clip_rim.at[side, r],
            send_sem=clip_send.at[side, r], recv_sem=clip_recv.at[side, r],
            device_id={"clip": clip - 1 if side == 1 else clip + 1}, device_id_type=MESH,
        )

    def convolve(r):
        total = base[r].astype(F32)
        for a in range(3):
            total = total + jnp.dot(swt[a], taps[r + a], preferred_element_type=F32)
        rounded = total.astype(BF16)
        spatial[r] = rounded
        wide = silu(norm_rows(rounded.astype(F32), gains[1])).astype(BF16)
        hidden[r] = wide
        wide = wide.astype(F32)
        first, last = wide[:, 0 : 2 * columns], wide[:, lanes - 2 * columns :]
        sent[1, r] = jnp.where(low, first[:half], swap(first[half:])).astype(BF16)
        sent[0, r] = jnp.where(low, swap(last[:half]), last[half:]).astype(BF16)
        pl.when(has_before)(lambda: clip_copy(1, r).start())
        pl.when(has_after)(lambda: clip_copy(0, r).start())

    def anchor_copy(slot, d, k, r, target):
        return pltpu.make_async_remote_copy(
            src_ref=anchors.at[slot, r], dst_ref=anchors.at[slot, r],
            send_sem=anchor_send.at[d * picks + k, r], recv_sem=anchor_recv.at[slot, r],
            device_id={"clip": target}, device_id_type=MESH,
        )

    def mix_frames(r):
        pl.when(has_before)(lambda: clip_copy(0, r).wait_recv())
        pl.when(has_after)(lambda: clip_copy(1, r).wait_recv())
        centre = hidden[r]
        wide = centre.astype(F32)
        before = clip_rim[0, r].astype(F32)
        after = clip_rim[1, r].astype(F32)
        before = jnp.where(has_before, jnp.concatenate([before, swap(before)], axis=0), 0.0)
        after = jnp.where(has_after, jnp.concatenate([swap(after), after], axis=0), 0.0)
        copies = lanes // (2 * columns)
        before = jnp.concatenate([before] * copies, axis=1)
        after = jnp.concatenate([after] * copies, axis=1)
        before = jnp.where(frame == 0, before, pltpu.roll(wide, columns, 1)).astype(BF16)
        after = jnp.where(frame == frames - 1, after, pltpu.roll(wide, lanes - columns, 1)).astype(BF16)
        stacked = jnp.concatenate([before, centre, after], axis=0)
        total = spatial[r].astype(F32) + jnp.dot(twt[...], stacked, preferred_element_type=F32)
        rounded = total.astype(BF16)
        temporal[r] = rounded
        normed = norm_rows(rounded.astype(F32), gains[2]).astype(BF16)
        wide = normed.astype(F32)
        for k in range(picks):
            pick = anchor_index[0, k]
            tile = wide[:, 0 : 2 * columns]
            for t in range(1, lanes // (2 * columns)):
                tile = jnp.where(pick >= 2 * t, wide[:, 2 * t * columns : 2 * (t + 1) * columns], tile)
            turned = swap(tile)
            odd = lax.rem(pick, 2) == 1
            upper = jnp.where(odd, turned[:half], tile[:half])
            lower = jnp.where(odd, tile[half:], turned[half:])
            slot = clip * picks + k
            anchors[slot, r] = jnp.where(low, upper, lower).astype(BF16)
            for d, other in enumerate(others):
                anchor_copy(slot, d, k, r, other).start()
        qkv[r] = jnp.dot(wqkvt[...], normed, preferred_element_type=F32).astype(BF16)

    def row_at(t):
        if rows < 3:
            return t
        return jnp.where(t < rows - 2, t + 1, jnp.where(t == rows - 2, 0, rows - 1))

    lag = 2

    @pl.loop(0, rows + lag)
    def _(t):
        @pl.when(t == max(rows - 2, 0))
        def _():
            put_rim(0, 0, has_up)
            put_rim(1, rows + 1, has_down)

        pl.when(t < rows)(lambda: convolve(row_at(t)))
        pl.when(t >= lag)(lambda: mix_frames(row_at(t - lag)))

    scale = 1.0 / math.sqrt(HEAD_DIM)
    groups = clips * picks // frames
    reach = window[0]

    def attend(r):
        for o in others:
            for k in range(picks):
                anchor_copy(o * picks + k, 0, k, r, o).wait_recv()
        keys = [qkv[r, channels : 2 * channels].astype(F32)]
        values = [qkv[r, 2 * channels :].astype(F32)]
        for g in range(groups):
            tiles = []
            for t in range(frames // 2):
                left = anchors[g * frames + 2 * t, r].astype(F32)
                right = anchors[g * frames + 2 * t + 1, r].astype(F32)
                upper = jnp.where(low, left, swap(right))
                lower = jnp.where(low, swap(left), right)
                tiles.append(jnp.concatenate([upper, lower], axis=0))
            normed = jnp.concatenate(tiles, axis=1).astype(BF16)
            both = jnp.dot(wqkvt[channels:], normed, preferred_element_type=F32).astype(BF16).astype(F32)
            keys.append(both[:channels])
            values.append(both[channels:])
        query = qkv[r, 0:channels].astype(F32)
        parts = []
        for h in range(heads):
            span = slice(h * HEAD_DIM, (h + 1) * HEAD_DIM)
            mine = query[span]
            scores = []
            for g, key in enumerate(keys):
                for step in range(frames):
                    moved = key[span]
                    if step:
                        moved = pltpu.roll(moved, lanes - step * columns, 1)
                    score = jnp.sum(mine * moved, axis=0, keepdims=True) * scale
                    if g == 0 and step:
                        away = jnp.abs(frame - lax.rem(frame + step, frames))
                        score = jnp.where(away < reach, score, -jnp.inf)
                    scores.append(score)
            top = functools.reduce(jnp.maximum, scores)
            weights = [jnp.exp(score - top) for score in scores]
            norm = functools.reduce(jnp.add, weights)
            mixed = jnp.zeros((HEAD_DIM, lanes), F32)
            for n, weight in enumerate(weights):
                prob = (weight / norm).astype(BF16).astype(F32)
                moved = values[n // frames][span]
                if n % frames:
                    moved = pltpu.roll(moved, lanes - (n % frames) * columns, 1)
                mixed = mixed + prob * moved
            parts.append(mixed.astype(BF16))
        attended = jnp.concatenate(parts, axis=0)
        total = temporal[r].astype(F32) + jnp.dot(wot[...], attended, preferred_element_type=F32)
        out[:, r] = total.T.reshape(frames, columns, channels).astype(out.dtype)

    @pl.loop(0, rows)
    def _(t):
        attend(row_at(t))

    pl.when(has_up)(lambda: rim_copy(1).wait_send())
    pl.when(has_down)(lambda: rim_copy(0).wait_send())

    @pl.loop(0, rows)
    def _(r):
        pl.when(has_before)(lambda: clip_copy(1, r).wait_send())
        pl.when(has_after)(lambda: clip_copy(0, r).wait_send())
        for d, other in enumerate(others):
            for k in range(picks):
                anchor_copy(clip * picks + k, d, k, r, other).wait_send()


def on_device(mesh, *args):
    latents, anchor_index = args[0], args[1]
    frames, rows, columns, channels = latents.shape
    strips, clips = mesh.shape["strip"], mesh.shape["clip"]
    picks = anchor_index.shape[1]
    lanes = frames * columns
    half = channels // 2
    assert frames % 2 == 0 and (clips * picks) % frames == 0
    dims = (frames, rows, columns, channels, strips, clips, picks)
    anywhere = pl.BlockSpec(memory_space=pl.ANY)
    vmem = pl.BlockSpec(memory_space=pltpu.VMEM)
    smem = pl.BlockSpec(memory_space=pltpu.SMEM)
    dma = pltpu.SemaphoreType.DMA
    args = [a.reshape(1, -1) if i in (3, 5, 7) else a for i, a in enumerate(args)]
    slots = clips * picks
    return pl.pallas_call(
        functools.partial(kernel, dims),
        out_shape=jax.ShapeDtypeStruct(latents.shape, latents.dtype),
        in_specs=[anywhere, smem, smem, vmem, anywhere, vmem, anywhere, vmem, anywhere, anywhere, anywhere],
        out_specs=vmem,
        scratch_shapes=[
            pltpu.VMEM(latents.shape, BF16),
            pltpu.VMEM(args[4].shape, BF16),
            pltpu.VMEM(args[6].shape, BF16),
            pltpu.VMEM(args[8].shape, BF16),
            pltpu.VMEM(args[9].shape, BF16),
            pltpu.VMEM(args[10].shape, BF16),
            pltpu.VMEM((3, channels, 3 * channels), BF16),
            pltpu.VMEM((channels, 3 * channels), BF16),
            pltpu.VMEM((3 * channels, channels), BF16),
            pltpu.VMEM((channels, channels), BF16),
            pltpu.VMEM((3, channels, lanes), F32),
            pltpu.VMEM((2, frames, columns, channels), BF16),
            pltpu.VMEM((rows + 2, 3 * channels, lanes), BF16),
            pltpu.VMEM((rows, channels, lanes), BF16),
            pltpu.VMEM((rows, channels, lanes), BF16),
            pltpu.VMEM((rows, channels, lanes), BF16),
            pltpu.VMEM((rows, channels, lanes), BF16),
            pltpu.VMEM((rows, 3 * channels, lanes), BF16),
            pltpu.VMEM((2, rows, half, 2 * columns), BF16),
            pltpu.VMEM((2, rows, half, 2 * columns), BF16),
            pltpu.VMEM((slots, rows, half, 2 * columns), BF16),
            dma((6,)),
            dma((2,)),
            dma((2,)),
            dma((2, rows)),
            dma((2, rows)),
            dma(((clips - 1) * picks, rows)),
            dma((slots, rows)),
        ],
        compiler_params=pltpu.CompilerParams(
            collective_id=0, has_side_effects=True, vmem_limit_bytes=60 * 2**20
        ),
        name="unet_block",
    )(*args)


def solution(mesh):
    return jax.shard_map(
        functools.partial(on_device, mesh),
        mesh=mesh,
        in_specs=(
            P(("groups", "clip"), "strip", None, None),
            P(("groups", "clip"), None),
            P(),
            P(),
            P(),
            P(),
            P(),
            P(),
            P(),
            P(),
            P(),
        ),
        out_specs=P(("groups", "clip"), "strip", None, None),
        check_vma=False,
    )
```

```python
import functools
import math

import jax
import jax.numpy as jnp
from jax import lax
from jax.experimental import pallas as pl
from jax.experimental.pallas import tpu as pltpu
from jax.sharding import PartitionSpec as P

HEAD_DIM = 64
MESH = pl.DeviceIdType.MESH
F32 = jnp.float32
BF16 = jnp.bfloat16


def norm_rows(values, gain):
    inv = 1.0 / values.shape[0]
    centred = values - jnp.sum(values, axis=0, keepdims=True) * inv
    variance = jnp.sum(centred * centred, axis=0, keepdims=True) * inv
    return centred * lax.rsqrt(variance + 1e-05) * gain


def silu(u):
    return u / (1.0 + jnp.exp(-u))


def kernel(
    dims,
    latents, anchor_index, window, gain_one, spatial_w, gain_two, temporal_w, gain_three,
    w_query, w_keyval, w_out,
    out,
    lat, sw, tw, wq, wkv, wo, swt, twt, wqkvt, wot, gains,
    rim, taps, base, spatial, hidden, temporal, qkv, sent, clip_rim, anchors,
    local_sem, rim_send, rim_recv, clip_send, clip_recv, anchor_send, anchor_recv, forward_send,
):
    frames, rows, columns, channels, strips, clips, picks = dims
    lanes = frames * columns
    half = channels // 2
    heads = channels // HEAD_DIM
    strip = lax.axis_index("strip")
    clip = lax.axis_index("clip")
    has_up, has_down = strip > 0, strip < strips - 1
    has_before, has_after = clip > 0, clip < clips - 1

    loads = [
        pltpu.make_async_copy(src, dst, local_sem.at[i])
        for i, (src, dst) in enumerate(
            ((latents, lat), (spatial_w, sw), (temporal_w, tw), (w_query, wq), (w_keyval, wkv), (w_out, wo))
        )
    ]
    for load in loads:
        load.start()

    barrier = pltpu.get_barrier_semaphore()

    @pl.when(has_up)
    def _():
        pl.semaphore_signal(barrier, inc=1, device_id={"strip": strip - 1}, device_id_type=MESH)

    @pl.when(has_down)
    def _():
        pl.semaphore_signal(barrier, inc=1, device_id={"strip": strip + 1}, device_id_type=MESH)

    others = [lax.rem(clip + d, clips) for d in range(1, clips)]
    for other in others:
        pl.semaphore_signal(barrier, inc=1, device_id={"clip": other}, device_id_type=MESH)

    def rim_copy(side):
        source = latents.at[:, 0] if side == 1 else latents.at[:, rows - 1]
        return pltpu.make_async_remote_copy(
            src_ref=source, dst_ref=rim.at[side], send_sem=rim_send.at[side], recv_sem=rim_recv.at[side],
            device_id={"strip": strip - 1 if side == 1 else strip + 1}, device_id_type=MESH,
        )

    lane = lax.broadcasted_iota(jnp.int32, (1, lanes), 1)
    column = lax.rem(lane, columns)
    frame = lane // columns
    lane_half = lax.broadcasted_iota(jnp.int32, (1, 2 * columns), 1)
    low = lane_half < columns

    for i, ref in enumerate((gain_one, gain_two, gain_three)):
        turned = jnp.broadcast_to(ref[...].reshape(1, channels), (8, channels)).T
        gains[i] = jnp.broadcast_to(turned[:, 0:1], (channels, lanes))

    def put_taps(slot, turned):
        wide = silu(norm_rows(turned, gains[0]))
        left = jnp.where(column == 0, 0.0, pltpu.roll(wide, 1, 1))
        right = jnp.where(column == columns - 1, 0.0, pltpu.roll(wide, lanes - 1, 1))
        taps[slot, 0:channels] = left.astype(BF16)
        taps[slot, channels : 2 * channels] = wide.astype(BF16)
        taps[slot, 2 * channels :] = right.astype(BF16)

    def prepare(r):
        turned = lat[:, r].reshape(lanes, channels).astype(F32).T
        base[r] = turned.astype(BF16)
        put_taps(r + 1, turned)

    loads[0].wait()
    pl.loop(0, 3)(prepare)
    loads[1].wait()
    for a in range(3):
        swt[a] = sw[a].reshape(3 * channels, channels).astype(F32).T.astype(BF16)

    pl.semaphore_wait(barrier, clips - 1 + has_up.astype(jnp.int32) + has_down.astype(jnp.int32))
    pl.when(has_up)(lambda: rim_copy(1).start())
    pl.when(has_down)(lambda: rim_copy(0).start())

    def put_rim(side, slot, present):
        @pl.when(present)
        def _():
            rim_copy(side).wait_recv()
            put_taps(slot, rim[side].reshape(lanes, channels).astype(F32).T)

        @pl.when(jnp.logical_not(present))
        def _():
            taps[slot] = jnp.zeros(taps.shape[1:], BF16)

    def swap(values):
        return pltpu.roll(values, columns, 1)

    def clip_copy(side, r):
        return pltpu.make_async_remote_copy(
            src_ref=sent.at[side, r], dst_ref=clip_rim.at[side, r],
            send_sem=clip_send.at[side, r], recv_sem=clip_recv.at[side, r],
            device_id={"clip": clip - 1 if side == 1 else clip + 1}, device_id_type=MESH,
        )

    def convolve(r):
        total = base[r].astype(F32)
        for a in range(3):
            total = total + jnp.dot(swt[a], taps[r + a], preferred_element_type=F32)
        rounded = total.astype(BF16)
        spatial[r] = rounded
        wide = silu(norm_rows(rounded.astype(F32), gains[1])).astype(BF16)
        hidden[r] = wide
        wide = wide.astype(F32)
        first, last = wide[:, 0 : 2 * columns], wide[:, lanes - 2 * columns :]
        sent[1, r] = jnp.where(low, first[:half], swap(first[half:])).astype(BF16)
        sent[0, r] = jnp.where(low, swap(last[:half]), last[half:]).astype(BF16)

    def convolve_send(r):
        pl.when(has_before)(lambda: clip_copy(1, r).start())
        pl.when(has_after)(lambda: clip_copy(0, r).start())

    def anchor_copy(slot, d, k, r, target):
        return pltpu.make_async_remote_copy(
            src_ref=anchors.at[slot, r], dst_ref=anchors.at[slot, r],
            send_sem=anchor_send.at[d * picks + k, r], recv_sem=anchor_recv.at[slot, r],
            device_id={"clip": target}, device_id_type=MESH,
        )

    def forward_copy(side, k, r):
        slot = (clip + 1 if side == 1 else clip - 1) * picks + k
        return pltpu.make_async_remote_copy(
            src_ref=anchors.at[slot, r], dst_ref=anchors.at[slot, r],
            send_sem=forward_send.at[side * picks + k, r], recv_sem=anchor_recv.at[slot, r],
            device_id={"clip": clip - 1 if side == 1 else clip + 1}, device_id_type=MESH,
        )

    def forward(r):
        for k in range(picks):
            for side, near, far in ((0, has_before, has_after), (1, has_after, has_before)):

                @pl.when(near)
                def _():
                    slot = (clip + 1 if side == 1 else clip - 1) * picks + k
                    target = clip + 1 if side == 1 else clip - 1
                    anchor_copy(slot, 0, k, r, target).wait_recv()

                pl.when(jnp.logical_and(near, far))(lambda: forward_copy(side, k, r).start())

    def mix_wait(r):
        pl.when(has_before)(lambda: clip_copy(0, r).wait_recv())
        pl.when(has_after)(lambda: clip_copy(1, r).wait_recv())

    def mix_send(r):
        for k in range(picks):
            for d, other in enumerate(others):
                direct = jnp.abs(other - clip) != 2
                pl.when(direct)(lambda: anchor_copy(clip * picks + k, d, k, r, other).start())

    def mix_frames(r):
        centre = hidden[r]
        wide = centre.astype(F32)
        before = clip_rim[0, r].astype(F32)
        after = clip_rim[1, r].astype(F32)
        before = jnp.where(has_before, jnp.concatenate([before, swap(before)], axis=0), 0.0)
        after = jnp.where(has_after, jnp.concatenate([swap(after), after], axis=0), 0.0)
        copies = lanes // (2 * columns)
        before = jnp.concatenate([before] * copies, axis=1)
        after = jnp.concatenate([after] * copies, axis=1)
        before = jnp.where(frame == 0, before, pltpu.roll(wide, columns, 1)).astype(BF16)
        after = jnp.where(frame == frames - 1, after, pltpu.roll(wide, lanes - columns, 1)).astype(BF16)
        stacked = jnp.concatenate([before, centre, after], axis=0)
        total = spatial[r].astype(F32) + jnp.dot(twt[...], stacked, preferred_element_type=F32)
        rounded = total.astype(BF16)
        temporal[r] = rounded
        normed = norm_rows(rounded.astype(F32), gains[2]).astype(BF16)
        wide = normed.astype(F32)
        for k in range(picks):
            pick = anchor_index[0, k]
            tile = wide[:, 0 : 2 * columns]
            for t in range(1, lanes // (2 * columns)):
                tile = jnp.where(pick >= 2 * t, wide[:, 2 * t * columns : 2 * (t + 1) * columns], tile)
            turned = swap(tile)
            odd = lax.rem(pick, 2) == 1
            upper = jnp.where(odd, turned[:half], tile[:half])
            lower = jnp.where(odd, tile[half:], turned[half:])
            slot = clip * picks + k
            anchors[slot, r] = jnp.where(low, upper, lower).astype(BF16)
        qkv[r] = jnp.dot(wqkvt[...], normed, preferred_element_type=F32).astype(BF16)

    def row_at(t):
        return jnp.where(t < rows - 2, t + 1, jnp.where(t == rows - 2, 0, rows - 1))

    lag = 2
    convolve(1)
    convolve_send(1)
    for load in loads[2:]:
        load.wait()
    twt[...] = tw[...].reshape(3 * channels, channels).astype(F32).T.astype(BF16)
    pl.loop(3, rows)(prepare)
    convolve(row_at(1))
    convolve_send(row_at(1))
    wqkvt[0:channels] = wq[...].astype(F32).T.astype(BF16)
    wqkvt[channels:] = wkv[...].astype(F32).T.astype(BF16)
    wot[...] = wo[...].astype(F32).T.astype(BF16)

    @pl.loop(lag, rows)
    def _(t):
        @pl.when(t == rows - 2)
        def _():
            put_rim(0, 0, has_up)
            put_rim(1, rows + 1, has_down)

        mix_wait(row_at(t - lag))
        mix_frames(row_at(t - lag))
        convolve(row_at(t))
        mix_send(row_at(t - lag))
        convolve_send(row_at(t))
        pl.when(t > lag)(lambda: forward(row_at(t - lag - 1)))

    @pl.loop(rows, rows + lag)
    def _(t):
        mix_wait(row_at(t - lag))
        mix_frames(row_at(t - lag))
        mix_send(row_at(t - lag))
        forward(row_at(t - lag - 1))

    scale = 1.0 / math.sqrt(HEAD_DIM)
    groups = clips * picks // frames
    reach = window[0]

    def attend(r):
        for o in others:
            for k in range(picks):
                distant = jnp.abs(o - clip) > 1
                pl.when(distant)(lambda: anchor_copy(o * picks + k, 0, k, r, o).wait_recv())
        keys = [qkv[r, channels : 2 * channels].astype(F32)]
        values = [qkv[r, 2 * channels :].astype(F32)]
        for g in range(groups):
            tiles = []
            for t in range(frames // 2):
                left = anchors[g * frames + 2 * t, r].astype(F32)
                right = anchors[g * frames + 2 * t + 1, r].astype(F32)
                upper = jnp.where(low, left, swap(right))
                lower = jnp.where(low, swap(left), right)
                tiles.append(jnp.concatenate([upper, lower], axis=0))
            normed = jnp.concatenate(tiles, axis=1).astype(BF16)
            both = jnp.dot(wqkvt[channels:], normed, preferred_element_type=F32).astype(BF16).astype(F32)
            keys.append(both[:channels])
            values.append(both[channels:])
        query = qkv[r, 0:channels].astype(F32)
        parts = []
        for h in range(heads):
            span = slice(h * HEAD_DIM, (h + 1) * HEAD_DIM)
            mine = query[span]
            scores = []
            for g, key in enumerate(keys):
                for step in range(frames):
                    moved = key[span]
                    if step:
                        moved = pltpu.roll(moved, lanes - step * columns, 1)
                    score = jnp.sum(mine * moved, axis=0, keepdims=True) * scale
                    if g == 0 and step:
                        away = jnp.abs(frame - lax.rem(frame + step, frames))
                        score = jnp.where(away < reach, score, -jnp.inf)
                    scores.append(score)
            top = functools.reduce(jnp.maximum, scores)
            weights = [jnp.exp(score - top) for score in scores]
            norm = functools.reduce(jnp.add, weights)
            mixed = jnp.zeros((HEAD_DIM, lanes), F32)
            for n, weight in enumerate(weights):
                prob = (weight / norm).astype(BF16).astype(F32)
                moved = values[n // frames][span]
                if n % frames:
                    moved = pltpu.roll(moved, lanes - (n % frames) * columns, 1)
                mixed = mixed + prob * moved
            parts.append(mixed.astype(BF16))
        attended = jnp.concatenate(parts, axis=0)
        total = temporal[r].astype(F32) + jnp.dot(wot[...], attended, preferred_element_type=F32)
        out[:, r] = total.T.reshape(frames, columns, channels).astype(out.dtype)

    @pl.loop(0, rows)
    def _(t):
        attend(row_at(t))
        pl.when(t == 0)(lambda: forward(row_at(rows - 1)))

    pl.when(has_up)(lambda: rim_copy(1).wait_send())
    pl.when(has_down)(lambda: rim_copy(0).wait_send())

    @pl.loop(0, rows)
    def _(r):
        pl.when(has_before)(lambda: clip_copy(1, r).wait_send())
        pl.when(has_after)(lambda: clip_copy(0, r).wait_send())
        for d, other in enumerate(others):
            for k in range(picks):
                direct = jnp.abs(other - clip) != 2
                pl.when(direct)(lambda: anchor_copy(clip * picks + k, d, k, r, other).wait_send())
        for k in range(picks):
            for side in range(2):
                both = jnp.logical_and(has_before, has_after)
                pl.when(both)(lambda: forward_copy(side, k, r).wait_send())


def on_device(mesh, *args):
    latents, anchor_index = args[0], args[1]
    frames, rows, columns, channels = latents.shape
    strips, clips = mesh.shape["strip"], mesh.shape["clip"]
    picks = anchor_index.shape[1]
    lanes = frames * columns
    half = channels // 2
    assert rows >= 4 and frames % 2 == 0 and (clips * picks) % frames == 0
    dims = (frames, rows, columns, channels, strips, clips, picks)
    anywhere = pl.BlockSpec(memory_space=pl.ANY)
    vmem = pl.BlockSpec(memory_space=pltpu.VMEM)
    smem = pl.BlockSpec(memory_space=pltpu.SMEM)
    dma = pltpu.SemaphoreType.DMA
    slots = clips * picks
    return pl.pallas_call(
        functools.partial(kernel, dims),
        out_shape=jax.ShapeDtypeStruct(latents.shape, latents.dtype),
        in_specs=[anywhere, smem, smem, vmem, anywhere, vmem, anywhere, vmem, anywhere, anywhere, anywhere],
        out_specs=vmem,
        scratch_shapes=[
            pltpu.VMEM(latents.shape, BF16),
            pltpu.VMEM(args[4].shape, BF16),
            pltpu.VMEM(args[6].shape, BF16),
            pltpu.VMEM(args[8].shape, BF16),
            pltpu.VMEM(args[9].shape, BF16),
            pltpu.VMEM(args[10].shape, BF16),
            pltpu.VMEM((3, channels, 3 * channels), BF16),
            pltpu.VMEM((channels, 3 * channels), BF16),
            pltpu.VMEM((3 * channels, channels), BF16),
            pltpu.VMEM((channels, channels), BF16),
            pltpu.VMEM((3, channels, lanes), F32),
            pltpu.VMEM((2, frames, columns, channels), BF16),
            pltpu.VMEM((rows + 2, 3 * channels, lanes), BF16),
            pltpu.VMEM((rows, channels, lanes), BF16),
            pltpu.VMEM((rows, channels, lanes), BF16),
            pltpu.VMEM((rows, channels, lanes), BF16),
            pltpu.VMEM((rows, channels, lanes), BF16),
            pltpu.VMEM((rows, 3 * channels, lanes), BF16),
            pltpu.VMEM((2, rows, half, 2 * columns), BF16),
            pltpu.VMEM((2, rows, half, 2 * columns), BF16),
            pltpu.VMEM((slots, rows, half, 2 * columns), BF16),
            dma((6,)),
            dma((2,)),
            dma((2,)),
            dma((2, rows)),
            dma((2, rows)),
            dma(((clips - 1) * picks, rows)),
            dma((slots, rows)),
            dma((2 * picks, rows)),
        ],
        compiler_params=pltpu.CompilerParams(
            collective_id=0, has_side_effects=True, vmem_limit_bytes=56 * 2**20
        ),
        name="unet_block",
    )(*args)


def solution(mesh):
    return jax.shard_map(
        functools.partial(on_device, mesh),
        mesh=mesh,
        in_specs=(
            P(("groups", "clip"), "strip", None, None),
            P(("groups", "clip"), None),
            P(),
            P(),
            P(),
            P(),
            P(),
            P(),
            P(),
            P(),
            P(),
        ),
        out_specs=P(("groups", "clip"), "strip", None, None),
        check_vma=False,
    )
```

```python
import functools
import math

import jax
import jax.numpy as jnp
from jax import lax
from jax.experimental import pallas as pl
from jax.experimental.pallas import tpu as pltpu
from jax.sharding import PartitionSpec as P

HEAD_DIM = 64
MESH = pl.DeviceIdType.MESH
F32 = jnp.float32
BF16 = jnp.bfloat16


def norm_rows(values, gain):
    inv = 1.0 / values.shape[0]
    centred = values - jnp.sum(values, axis=0, keepdims=True) * inv
    variance = jnp.sum(centred * centred, axis=0, keepdims=True) * inv
    return centred * lax.rsqrt(variance + 1e-05) * gain


def silu(u):
    return u / (1.0 + jnp.exp(-u))


def kernel(
    dims,
    latents, anchor_index, window, gain_one, spatial_w, gain_two, temporal_w, gain_three,
    w_query, w_keyval, w_out,
    out,
    lat, sw, tw, wq, wkv, wo, swt, twt, wqkvt, wot, gains,
    rim, taps, base, spatial, hidden, temporal, qkv, sent, clip_rim, anchors,
    local_sem, rim_send, rim_recv, clip_send, clip_recv, anchor_send, anchor_recv, forward_send,
):
    frames, rows, columns, channels, strips, clips, picks = dims
    lanes = frames * columns
    half = channels // 2
    heads = channels // HEAD_DIM
    strip = lax.axis_index("strip")
    clip = lax.axis_index("clip")
    has_up, has_down = strip > 0, strip < strips - 1
    has_before, has_after = clip > 0, clip < clips - 1

    loads = [
        pltpu.make_async_copy(src, dst, local_sem.at[i])
        for i, (src, dst) in enumerate(
            ((latents, lat), (spatial_w, sw), (temporal_w, tw), (w_query, wq), (w_keyval, wkv), (w_out, wo))
        )
    ]
    for load in loads:
        load.start()

    barrier = pltpu.get_barrier_semaphore()

    @pl.when(has_up)
    def _():
        pl.semaphore_signal(barrier, inc=1, device_id={"strip": strip - 1}, device_id_type=MESH)

    @pl.when(has_down)
    def _():
        pl.semaphore_signal(barrier, inc=1, device_id={"strip": strip + 1}, device_id_type=MESH)

    others = [lax.rem(clip + d, clips) for d in range(1, clips)]
    for other in others:
        pl.semaphore_signal(barrier, inc=1, device_id={"clip": other}, device_id_type=MESH)

    def rim_copy(side):
        source = latents.at[:, 0] if side == 1 else latents.at[:, rows - 1]
        return pltpu.make_async_remote_copy(
            src_ref=source, dst_ref=rim.at[side], send_sem=rim_send.at[side], recv_sem=rim_recv.at[side],
            device_id={"strip": strip - 1 if side == 1 else strip + 1}, device_id_type=MESH,
        )

    lane = lax.broadcasted_iota(jnp.int32, (1, lanes), 1)
    column = lax.rem(lane, columns)
    frame = lane // columns
    lane_half = lax.broadcasted_iota(jnp.int32, (1, 2 * columns), 1)
    low = lane_half < columns

    for i, ref in enumerate((gain_one, gain_two, gain_three)):
        turned = jnp.broadcast_to(ref[...].reshape(1, channels), (8, channels)).T
        gains[i] = jnp.broadcast_to(turned[:, 0:1], (channels, lanes))

    def put_taps(slot, turned):
        wide = silu(norm_rows(turned, gains[0]))
        left = jnp.where(column == 0, 0.0, pltpu.roll(wide, 1, 1))
        right = jnp.where(column == columns - 1, 0.0, pltpu.roll(wide, lanes - 1, 1))
        taps[slot, 0:channels] = left.astype(BF16)
        taps[slot, channels : 2 * channels] = wide.astype(BF16)
        taps[slot, 2 * channels :] = right.astype(BF16)

    def prepare(r):
        turned = lat[:, r].reshape(lanes, channels).astype(F32).T
        base[r] = turned.astype(BF16)
        put_taps(r + 1, turned)

    loads[0].wait()
    pl.loop(0, 3)(prepare)
    loads[1].wait()
    for a in range(3):
        swt[a] = sw[a].reshape(3 * channels, channels).astype(F32).T.astype(BF16)

    pl.semaphore_wait(barrier, clips - 1 + has_up.astype(jnp.int32) + has_down.astype(jnp.int32))
    pl.when(has_up)(lambda: rim_copy(1).start())
    pl.when(has_down)(lambda: rim_copy(0).start())

    def put_rim(side, slot, present):
        @pl.when(present)
        def _():
            rim_copy(side).wait_recv()
            put_taps(slot, rim[side].reshape(lanes, channels).astype(F32).T)

        @pl.when(jnp.logical_not(present))
        def _():
            taps[slot] = jnp.zeros(taps.shape[1:], BF16)

    def swap(values):
        return pltpu.roll(values, columns, 1)

    def clip_copy(side, r):
        return pltpu.make_async_remote_copy(
            src_ref=sent.at[side, r], dst_ref=clip_rim.at[side, r],
            send_sem=clip_send.at[side, r], recv_sem=clip_recv.at[side, r],
            device_id={"clip": clip - 1 if side == 1 else clip + 1}, device_id_type=MESH,
        )

    def convolve(r):
        total = base[r].astype(F32)
        for a in range(3):
            total = total + jnp.dot(swt[a], taps[r + a], preferred_element_type=F32)
        rounded = total.astype(BF16)
        spatial[r] = rounded
        wide = silu(norm_rows(rounded.astype(F32), gains[1])).astype(BF16)
        hidden[r] = wide
        wide = wide.astype(F32)
        first, last = wide[:, 0 : 2 * columns], wide[:, lanes - 2 * columns :]
        sent[1, r] = jnp.where(low, first[:half], swap(first[half:])).astype(BF16)
        sent[0, r] = jnp.where(low, swap(last[:half]), last[half:]).astype(BF16)

    def convolve_send(r):
        pl.when(has_before)(lambda: clip_copy(1, r).start())
        pl.when(has_after)(lambda: clip_copy(0, r).start())

    def anchor_copy(slot, d, k, r, target):
        return pltpu.make_async_remote_copy(
            src_ref=anchors.at[slot, r], dst_ref=anchors.at[slot, r],
            send_sem=anchor_send.at[d * picks + k, r], recv_sem=anchor_recv.at[slot, r],
            device_id={"clip": target}, device_id_type=MESH,
        )

    def forward_copy(side, k, r):
        slot = (clip + 1 if side == 1 else clip - 1) * picks + k
        return pltpu.make_async_remote_copy(
            src_ref=anchors.at[slot, r], dst_ref=anchors.at[slot, r],
            send_sem=forward_send.at[side * picks + k, r], recv_sem=anchor_recv.at[slot, r],
            device_id={"clip": clip - 1 if side == 1 else clip + 1}, device_id_type=MESH,
        )

    def forward(r):
        for k in range(picks):
            for side, near, far in ((0, has_before, has_after), (1, has_after, has_before)):

                @pl.when(near)
                def _():
                    slot = (clip + 1 if side == 1 else clip - 1) * picks + k
                    target = clip + 1 if side == 1 else clip - 1
                    anchor_copy(slot, 0, k, r, target).wait_recv()

                pl.when(jnp.logical_and(near, far))(lambda: forward_copy(side, k, r).start())

    def mix_wait(r):
        pl.when(has_before)(lambda: clip_copy(0, r).wait_recv())
        pl.when(has_after)(lambda: clip_copy(1, r).wait_recv())

    def mix_send(r):
        for k in range(picks):
            for d, other in enumerate(others):
                direct = jnp.abs(other - clip) != 2
                pl.when(direct)(lambda: anchor_copy(clip * picks + k, d, k, r, other).start())

    def mix_frames(r):
        centre = hidden[r]
        wide = centre.astype(F32)
        before = clip_rim[0, r].astype(F32)
        after = clip_rim[1, r].astype(F32)
        before = jnp.where(has_before, jnp.concatenate([before, swap(before)], axis=0), 0.0)
        after = jnp.where(has_after, jnp.concatenate([swap(after), after], axis=0), 0.0)
        copies = lanes // (2 * columns)
        before = jnp.concatenate([before] * copies, axis=1)
        after = jnp.concatenate([after] * copies, axis=1)
        before = jnp.where(frame == 0, before, pltpu.roll(wide, columns, 1)).astype(BF16)
        after = jnp.where(frame == frames - 1, after, pltpu.roll(wide, lanes - columns, 1)).astype(BF16)
        stacked = jnp.concatenate([before, centre, after], axis=0)
        total = spatial[r].astype(F32) + jnp.dot(twt[...], stacked, preferred_element_type=F32)
        rounded = total.astype(BF16)
        temporal[r] = rounded
        normed = norm_rows(rounded.astype(F32), gains[2]).astype(BF16)
        wide = normed.astype(F32)
        for k in range(picks):
            pick = anchor_index[0, k]
            tile = wide[:, 0 : 2 * columns]
            for t in range(1, lanes // (2 * columns)):
                tile = jnp.where(pick >= 2 * t, wide[:, 2 * t * columns : 2 * (t + 1) * columns], tile)
            turned = swap(tile)
            odd = lax.rem(pick, 2) == 1
            upper = jnp.where(odd, turned[:half], tile[:half])
            lower = jnp.where(odd, tile[half:], turned[half:])
            slot = clip * picks + k
            anchors[slot, r] = jnp.where(low, upper, lower).astype(BF16)
        qkv[r] = jnp.dot(wqkvt[...], normed, preferred_element_type=F32).astype(BF16)

    def row_at(t):
        return jnp.where(t < rows - 2, t + 1, jnp.where(t == rows - 2, 0, rows - 1))

    lag = 3
    delay = 2
    convolve(1)
    convolve_send(1)
    for load in loads[2:]:
        load.wait()
    twt[...] = tw[...].reshape(3 * channels, channels).astype(F32).T.astype(BF16)
    pl.loop(3, rows)(prepare)
    convolve(row_at(1))
    convolve_send(row_at(1))
    wqkvt[0:channels] = wq[...].astype(F32).T.astype(BF16)
    wqkvt[channels:] = wkv[...].astype(F32).T.astype(BF16)
    wot[...] = wo[...].astype(F32).T.astype(BF16)
    for t in range(2, lag):
        convolve(row_at(t))
        convolve_send(row_at(t))

    @pl.loop(lag, rows)
    def _(t):
        @pl.when(t == rows - 2)
        def _():
            put_rim(0, 0, has_up)
            put_rim(1, rows + 1, has_down)

        mix_wait(row_at(t - lag))
        mix_frames(row_at(t - lag))
        mix_send(row_at(t - lag))
        convolve(row_at(t))
        convolve_send(row_at(t))
        pl.when(t >= lag + delay)(lambda: forward(row_at(t - lag - delay)))

    @pl.loop(rows, rows + lag)
    def _(t):
        mix_wait(row_at(t - lag))
        mix_frames(row_at(t - lag))
        mix_send(row_at(t - lag))
        pl.when(t >= lag + delay)(lambda: forward(row_at(t - lag - delay)))

    scale = 1.0 / math.sqrt(HEAD_DIM)
    groups = clips * picks // frames
    reach = window[0]

    def attend(r):
        for o in others:
            for k in range(picks):
                distant = jnp.abs(o - clip) > 1
                pl.when(distant)(lambda: anchor_copy(o * picks + k, 0, k, r, o).wait_recv())
        keys = [qkv[r, channels : 2 * channels].astype(F32)]
        values = [qkv[r, 2 * channels :].astype(F32)]
        for g in range(groups):
            tiles = []
            for t in range(frames // 2):
                left = anchors[g * frames + 2 * t, r].astype(F32)
                right = anchors[g * frames + 2 * t + 1, r].astype(F32)
                upper = jnp.where(low, left, swap(right))
                lower = jnp.where(low, swap(left), right)
                tiles.append(jnp.concatenate([upper, lower], axis=0))
            normed = jnp.concatenate(tiles, axis=1).astype(BF16)
            both = jnp.dot(wqkvt[channels:], normed, preferred_element_type=F32).astype(BF16).astype(F32)
            keys.append(both[:channels])
            values.append(both[channels:])
        query = qkv[r, 0:channels].astype(F32)
        parts = []
        for h in range(heads):
            span = slice(h * HEAD_DIM, (h + 1) * HEAD_DIM)
            mine = query[span]
            scores = []
            for g, key in enumerate(keys):
                for step in range(frames):
                    moved = key[span]
                    if step:
                        moved = pltpu.roll(moved, lanes - step * columns, 1)
                    score = jnp.sum(mine * moved, axis=0, keepdims=True) * scale
                    if g == 0 and step:
                        away = jnp.abs(frame - lax.rem(frame + step, frames))
                        score = jnp.where(away < reach, score, -jnp.inf)
                    scores.append(score)
            top = functools.reduce(jnp.maximum, scores)
            weights = [jnp.exp(score - top) for score in scores]
            norm = functools.reduce(jnp.add, weights)
            mixed = jnp.zeros((HEAD_DIM, lanes), F32)
            for n, weight in enumerate(weights):
                prob = (weight / norm).astype(BF16).astype(F32)
                moved = values[n // frames][span]
                if n % frames:
                    moved = pltpu.roll(moved, lanes - (n % frames) * columns, 1)
                mixed = mixed + prob * moved
            parts.append(mixed.astype(BF16))
        attended = jnp.concatenate(parts, axis=0)
        total = temporal[r].astype(F32) + jnp.dot(wot[...], attended, preferred_element_type=F32)
        out[:, r] = total.T.reshape(frames, columns, channels).astype(out.dtype)

    @pl.loop(0, rows)
    def _(t):
        attend(row_at(t))
        pl.when(t < delay)(lambda: forward(row_at(t + rows - delay)))

    pl.when(has_up)(lambda: rim_copy(1).wait_send())
    pl.when(has_down)(lambda: rim_copy(0).wait_send())

    @pl.loop(0, rows)
    def _(r):
        pl.when(has_before)(lambda: clip_copy(1, r).wait_send())
        pl.when(has_after)(lambda: clip_copy(0, r).wait_send())
        for d, other in enumerate(others):
            for k in range(picks):
                direct = jnp.abs(other - clip) != 2
                pl.when(direct)(lambda: anchor_copy(clip * picks + k, d, k, r, other).wait_send())
        for k in range(picks):
            for side in range(2):
                both = jnp.logical_and(has_before, has_after)
                pl.when(both)(lambda: forward_copy(side, k, r).wait_send())


def on_device(mesh, *args):
    latents, anchor_index = args[0], args[1]
    frames, rows, columns, channels = latents.shape
    strips, clips = mesh.shape["strip"], mesh.shape["clip"]
    picks = anchor_index.shape[1]
    lanes = frames * columns
    half = channels // 2
    assert rows >= 4 and frames % 2 == 0 and (clips * picks) % frames == 0
    dims = (frames, rows, columns, channels, strips, clips, picks)
    anywhere = pl.BlockSpec(memory_space=pl.ANY)
    vmem = pl.BlockSpec(memory_space=pltpu.VMEM)
    smem = pl.BlockSpec(memory_space=pltpu.SMEM)
    dma = pltpu.SemaphoreType.DMA
    slots = clips * picks
    return pl.pallas_call(
        functools.partial(kernel, dims),
        out_shape=jax.ShapeDtypeStruct(latents.shape, latents.dtype),
        in_specs=[anywhere, smem, smem, vmem, anywhere, vmem, anywhere, vmem, anywhere, anywhere, anywhere],
        out_specs=vmem,
        scratch_shapes=[
            pltpu.VMEM(latents.shape, BF16),
            pltpu.VMEM(args[4].shape, BF16),
            pltpu.VMEM(args[6].shape, BF16),
            pltpu.VMEM(args[8].shape, BF16),
            pltpu.VMEM(args[9].shape, BF16),
            pltpu.VMEM(args[10].shape, BF16),
            pltpu.VMEM((3, channels, 3 * channels), BF16),
            pltpu.VMEM((channels, 3 * channels), BF16),
            pltpu.VMEM((3 * channels, channels), BF16),
            pltpu.VMEM((channels, channels), BF16),
            pltpu.VMEM((3, channels, lanes), F32),
            pltpu.VMEM((2, frames, columns, channels), BF16),
            pltpu.VMEM((rows + 2, 3 * channels, lanes), BF16),
            pltpu.VMEM((rows, channels, lanes), BF16),
            pltpu.VMEM((rows, channels, lanes), BF16),
            pltpu.VMEM((rows, channels, lanes), BF16),
            pltpu.VMEM((rows, channels, lanes), BF16),
            pltpu.VMEM((rows, 3 * channels, lanes), BF16),
            pltpu.VMEM((2, rows, half, 2 * columns), BF16),
            pltpu.VMEM((2, rows, half, 2 * columns), BF16),
            pltpu.VMEM((slots, rows, half, 2 * columns), BF16),
            dma((6,)),
            dma((2,)),
            dma((2,)),
            dma((2, rows)),
            dma((2, rows)),
            dma(((clips - 1) * picks, rows)),
            dma((slots, rows)),
            dma((2 * picks, rows)),
        ],
        compiler_params=pltpu.CompilerParams(
            collective_id=0, has_side_effects=True, vmem_limit_bytes=56 * 2**20
        ),
        name="unet_block",
    )(*args)


def solution(mesh):
    return jax.shard_map(
        functools.partial(on_device, mesh),
        mesh=mesh,
        in_specs=(
            P(("groups", "clip"), "strip", None, None),
            P(("groups", "clip"), None),
            P(),
            P(),
            P(),
            P(),
            P(),
            P(),
            P(),
            P(),
            P(),
        ),
        out_specs=P(("groups", "clip"), "strip", None, None),
        check_vma=False,
    )
```
